32 devices in a mesh: col: 8 (over y, x, core), row: 4 (over z).
Axes of the slice: x: 2, y: 2, z: 4, core: 2. Of those that a mesh axis runs over, the one named last changes fastest.
Arguments:
- rhs: bfloat16 [6, 8, 4, 128, 512], P(None, 'col', 'row'), may hold values from -6 to 6
- diag_inv: bfloat16 [6, 8, 4, 128, 128], P(None, 'col', 'row'), may hold values from -0.5 to 0.5
- factor: bfloat16 [5, 8, 4, 8, 2, 128, 128], P(None, 'col', 'row'), may hold values from -0.1875 to 0.1875
- columns: int32 [5, 8, 4, 8, 2], P(None, 'col', 'row'), may hold values from 0 to 3, as said below
Outputs:
- solution: bfloat16 [6, 8, 4, 128, 512], P(None, 'col', 'row')
The draws below stay inside these ranges and needn't reach their ends.
Inputs may be any that keep to these rules, and one draw needn't show every extreme that they name: The 2 entries of columns for one factor row block and one column owner are distinct.
All inputs are finite; a program needn't handle non-finite values.
Results may differ from the reference program's by a relative error of at most 0.025.
Values may be sent and summed in bfloat16 or wider, within the bound.
A program may use at most 128 MiB of HBM per device.

```python
import jax
import jax.numpy as jnp
from jax import lax

BLK = 128
NRHS = 512
STEPS = 6
SLOTS = 2
N_COL = 8
N_ROW = 4


def draw_columns(key, part):
    shape = (STEPS - 1, N_COL, N_ROW, N_COL, N_ROW)
    scores = jax.random.randint(jax.random.fold_in(key, 17), shape, 0, 1000)
    scores = scores * N_ROW + jnp.arange(N_ROW, dtype=jnp.int32)
    order = jnp.argsort(scores, axis=-1)
    return order[..., :SLOTS].astype(jnp.int32)


def spiked(result, stream_key, source, target, parts, factor):
    owner, partner = [(jnp.arange(result.shape[dim]) // (result.shape[dim] // parts)).reshape([-1 if axis == dim else 1 for axis in range(result.ndim)]) for dim in (source, target)]
    chosen = jax.random.permutation(stream_key, parts)[partner]
    strong = (owner == chosen) | (owner == (partner + parts // 2) % parts)
    return jnp.where(strong, factor * result, result)


def levels(stream_key, dims, shards, low, largest):
    level = 1.0
    for position, parts in shards:
        steps = jax.random.uniform(jax.random.fold_in(jax.random.fold_in(stream_key, 6), position), (parts,), jnp.float32, low / len(shards), largest / len(shards))
        level = level * jnp.repeat(jnp.exp(steps), dims[position] // parts).reshape((-1,) + (1,) * (len(dims) - 1 - position))
    return level


def gaussian(rng, extent, spread, most, split=(), kind=jnp.bfloat16):
    loudness = levels(rng, extent, split, -0.22, 0.18) if split else 1.0
    array = jax.random.normal(rng, extent, jnp.float32) * spread * loudness
    return jnp.minimum(jnp.maximum(array, -most), most).astype(kind)


def bell_draw_with(stream_key, dims, spread, bound, shards, heavy, held_as=jnp.bfloat16):
    entries = spread * jax.random.normal(stream_key, dims, jnp.float32)
    if shards:
        entries = entries * levels(stream_key, dims, shards, -0.22, 0.18)
    return jnp.clip(spiked(entries, jax.random.fold_in(stream_key, 3), *heavy), -bound, bound).astype(held_as)


def setup_inputs(seed: int = 0) -> dict:
    key_of = jax.random.split(jax.random.key(seed), 5)
    return {
        "rhs": gaussian(key_of[0], (STEPS, N_COL, N_ROW, BLK, NRHS), 1.0, 6.0, ((1, 8), (2, 4))),
        "diag_inv": gaussian(key_of[1], (STEPS, N_COL, N_ROW, BLK, BLK), BLK ** -0.5, 0.5, ((1, 8), (2, 4))),
        "factor": bell_draw_with(key_of[2], (STEPS - 1, N_COL, N_ROW, N_COL, SLOTS, BLK, BLK), (N_COL * SLOTS * BLK) ** -0.5, 0.1875, ((1, 8), (2, 4)), (1, 3, 8, 2.0)),
        "columns": draw_columns(jax.random.fold_in(key_of[4], 71), 0),
    }


def reference(rhs, diag_inv, factor, columns):
    highest = lax.Precision.HIGHEST
    remainder = rhs[0].astype(jnp.float32)
    solved = []
    for step_index in range(STEPS):
        current = jnp.einsum('crab,crbn->cran', diag_inv[step_index].astype(jnp.float32), remainder, precision=highest).astype(jnp.bfloat16)
        solved.append(current)
        if step_index + 1 < STEPS:
            def add_owner(carry, inputs):
                blocks, selected, panels = inputs
                chosen = jnp.take(panels, selected, axis=0).astype(jnp.float32)
                part_sum = jnp.einsum('rtmab,rtmbn->rtan', blocks.astype(jnp.float32), chosen, precision=highest)
                rounded = lax.optimization_barrier(part_sum.astype(jnp.bfloat16))
                return carry + rounded.astype(jnp.float32), None

            start_sum = jnp.zeros((N_ROW, N_COL, BLK, NRHS), jnp.float32)
            total, unused = lax.scan(add_owner, start_sum, (factor[step_index], columns[step_index], current))
            remainder = rhs[step_index + 1].astype(jnp.float32) - jnp.transpose(total, (1, 0, 2, 3))
    return jnp.stack(solved)
```

```python
import functools

import jax
import jax.numpy as jnp
from jax import lax
from jax.experimental import pallas as pl
from jax.experimental.pallas import tpu as pltpu
from jax.sharding import PartitionSpec as P

MESH = pl.DeviceIdType.MESH
CHUNKS = 2


def kernel(n_col, n_row, rhs, diag, fac, cols, cols_hbm, out, *scratch):
    steps, rows, width = rhs.shape[0], rhs.shape[3], rhs.shape[4]
    slots = fac.shape[4]
    chips = n_col // 2
    half = width // 2
    wide = half // CHUNKS
    links = steps - 1

    (rv, dv, fv, cp, own, sent, landed, last,
     in_loc, in_send, in_recv, z_send, z_recv, c_send, c_recv,
     o_loc, o_send, o_recv) = scratch[:18]
    panels = scratch[18:]

    col = lax.axis_index("col")
    row = lax.axis_index("row")
    core = lax.rem(col, 2)
    chip = lax.div(col, 2)
    partner = col + 1 - 2 * core
    mine = pl.ds(pl.multiple_of(core * half, half), half)
    theirs = pl.ds(pl.multiple_of((1 - core) * half, half), half)

    def to(c, r):
        return {"col": c, "row": r}

    def spans(total):
        return [pl.ds(0, 1), pl.ds(1, total - 1)]

    local = {}
    for g in range(2):
        a, b = spans(steps)[g], spans(links)[g]
        local["rhs", g] = pltpu.make_async_copy(rhs.at[a, 0, 0, :, mine], rv.at[a, 0], in_loc.at[0, g])
        local["diag", g] = pltpu.make_async_copy(diag.at[a, 0, 0], dv.at[a, 0], in_loc.at[1, g])
        local["fac", g] = pltpu.make_async_copy(fac.at[b, 0, 0], fv.at[b, 0], in_loc.at[2, g])
    for c in local.values():
        c.start()

    barrier = pltpu.get_barrier_semaphore()
    pl.semaphore_signal(barrier, inc=1, device_id=to(partner, row), device_id_type=MESH)
    for d in range(1, n_row):
        pl.semaphore_signal(barrier, inc=1, device_id=to(col, lax.rem(row + d, n_row)), device_id_type=MESH)
    for d in range(1, chips):
        other = lax.rem(chip + d, chips) * 2 + core
        pl.semaphore_signal(barrier, inc=1, device_id=to(other, row), device_id_type=MESH)
    pl.semaphore_wait(barrier, 1 + n_row - 1 + chips - 1)

    def remote(src, dst, send, recv, device):
        return pltpu.make_async_remote_copy(
            src_ref=src, dst_ref=dst, send_sem=send, recv_sem=recv,
            device_id=device, device_id_type=MESH)

    pair = to(partner, row)
    cross = {}
    for g in range(2):
        a, b = spans(steps)[g], spans(links)[g]
        cross["rhs", g] = remote(rhs.at[a, 0, 0, :, theirs], rv.at[a, 1], in_send.at[0, g], in_recv.at[0, g], pair)
        cross["diag", g] = remote(diag.at[a, 0, 0], dv.at[a, 1], in_send.at[1, g], in_recv.at[1, g], pair)
        cross["fac", g] = remote(fac.at[b, 0, 0], fv.at[b, 1], in_send.at[2, g], in_recv.at[2, g], pair)
        if g == 0:
            cross["cols", g] = remote(cols_hbm, cp, in_send.at[3, g], in_recv.at[3, g], pair)
    for c in cross.values():
        c.start()

    def arrived(name, g):
        if (name, g) in local:
            local[name, g].wait()
        cross[name, g].wait_recv()

    def part(ch):
        return pl.ds(ch * wide, wide)

    def z_copy(s, ch, d):
        buf = panels[s * CHUNKS + ch]
        return remote(buf.at[row], buf.at[row], z_send.at[s, ch, d - 1], z_recv.at[s, ch, d - 1],
                      to(col, lax.rem(row + d, n_row)))

    def c_copy(s, ch, d):
        other = lax.rem(chip + d, chips) * 2 + core
        return remote(sent.at[s, ch, d - 1], landed.at[s, ch, d - 1], c_send.at[s, ch, d - 1],
                      c_recv.at[s, ch, d - 1], to(other, row))

    def held(s, ch):
        return panels[s * CHUNKS + ch].at[row] if s < links else last.at[ch]

    def out_copies(s, ch):
        span = pl.ds(pl.multiple_of(core * half + ch * wide, wide), wide)
        src = held(s, ch)
        keep = pltpu.make_async_copy(src.at[0], out.at[s, 0, 0, :, span], o_loc.at[s, ch])
        give = remote(src.at[1], out.at[s, 0, 0, :, span], o_send.at[s, ch], o_recv.at[s, ch], pair)
        return keep, give

    def solve(s, ch):
        if s > 0:
            for d in range(1, chips):
                c_copy(s - 1, ch, d).wait_recv()
        for k in range(2):
            block = dv[s, k]
            right = rv[s, k, :, part(ch)]
            if s == 0:
                x = jnp.dot(block, right, preferred_element_type=jnp.float32)
            else:
                total = own[ch, k]
                for d in range(1, chips):
                    total = total + landed[s - 1, ch, d - 1, k].astype(jnp.float32)
                rem = right.astype(jnp.float32) - total
                high = rem.astype(jnp.bfloat16)
                low = (rem - high.astype(jnp.float32)).astype(jnp.bfloat16)
                x = jnp.dot(jnp.concatenate([block, block], axis=1),
                            jnp.concatenate([high, low], axis=0),
                            preferred_element_type=jnp.float32)
            x = x.astype(jnp.bfloat16)
            if s < links:
                panels[s * CHUNKS + ch][row, k] = x
            else:
                last[ch, k] = x
        if s < links:
            for d in range(1, n_row):
                z_copy(s, ch, d).start()
        for c in out_copies(s, ch):
            c.start()

    def term(s, ch, other, k):
        buf = panels[s * CHUNKS + ch]
        t = other * 2 + (core if k == 0 else 1 - core)
        left, right = [], []
        for slot, index in ((0, cols), (1, cp)):
            for m in range(slots):
                left.append(fv[s, slot, t, m])
                right.append(buf[index[s, 0, 0, t, m], slot])
        return jnp.dot(jnp.concatenate(left, axis=1), jnp.concatenate(right, axis=0),
                       preferred_element_type=jnp.float32)

    def spread(s, ch):
        for d in range(1, n_row):
            z_copy(s, ch, d).wait_recv()

        def one(d):
            other = lax.rem(chip + d, chips)
            for k in range(2):
                sent[s, ch, d - 1, k] = term(s, ch, other, k).astype(jnp.bfloat16)
            c_copy(s, ch, d).start()

        if chips <= 4:
            for d in range(1, chips):
                one(d)
        else:
            @pl.loop(1, chips)
            def _(d):
                one(d)
        for k in range(2):
            own[ch, k] = term(s, ch, chip, k)

    for s in range(steps):
        if s < 2:
            arrived("rhs", s)
            arrived("diag", s)
        for ch in range(CHUNKS):
            solve(s, ch)
        if s < 2:
            arrived("fac", s)
            if s == 0:
                arrived("cols", 0)
        if s < links:
            for ch in range(CHUNKS):
                spread(s, ch)

    for c in cross.values():
        c.wait_send()
    for s in range(steps):
        for ch in range(CHUNKS):
            keep, give = out_copies(s, ch)
            keep.wait()
            give.wait()
            if s < links:
                for d in range(1, n_row):
                    z_copy(s, ch, d).wait_send()
                for d in range(1, chips):
                    c_copy(s, ch, d).wait_send()


def on_device(n_col, n_row, rhs, diag_inv, factor, columns):
    steps, rows, width = rhs.shape[0], rhs.shape[3], rhs.shape[4]
    targets, slots = factor.shape[3], factor.shape[4]
    chips, half = n_col // 2, width // 2
    wide, links = half // CHUNKS, steps - 1
    bf16 = jnp.bfloat16
    dma = pltpu.SemaphoreType.DMA
    scratch = [
        pltpu.VMEM((steps, 2, rows, half), bf16),
        pltpu.VMEM((steps, 2, rows, rows), bf16),
        pltpu.VMEM((links, 2, targets, slots, rows, rows), bf16),
        pltpu.SMEM(columns.shape, jnp.int32),
        pltpu.VMEM((CHUNKS, 2, rows, wide), jnp.float32),
        pltpu.VMEM((links, CHUNKS, chips - 1, 2, rows, wide), bf16),
        pltpu.VMEM((links, CHUNKS, chips - 1, 2, rows, wide), bf16),
        pltpu.VMEM((CHUNKS, 2, rows, wide), bf16),
        dma((3, 2)), dma((4, 2)), dma((4, 2)),
        dma((links, CHUNKS, n_row - 1)), dma((links, CHUNKS, n_row - 1)),
        dma((links, CHUNKS, chips - 1)), dma((links, CHUNKS, chips - 1)),
        dma((steps, CHUNKS)), dma((steps, CHUNKS)), dma((steps, CHUNKS)),
    ] + [pltpu.VMEM((n_row, 2, rows, wide), bf16) for _ in range(links * CHUNKS)]
    anywhere = pl.BlockSpec(memory_space=pl.ANY)
    return pl.pallas_call(
        functools.partial(kernel, n_col, n_row),
        out_shape=jax.ShapeDtypeStruct(rhs.shape, bf16),
        in_specs=[anywhere, anywhere, anywhere, pl.BlockSpec(memory_space=pltpu.SMEM), anywhere],
        out_specs=anywhere,
        scratch_shapes=scratch,
        compiler_params=pltpu.CompilerParams(
            collective_id=0, has_side_effects=True, vmem_limit_bytes=60 * 1024 * 1024),
        name="levels",
    )(rhs, diag_inv, factor, columns, columns)


def solution(mesh):
    n_col, n_row = mesh.shape["col"], mesh.shape["row"]
    return jax.shard_map(
        functools.partial(on_device, n_col, n_row),
        mesh=mesh,
        in_specs=(
            P(None, "col", "row", None, None),
            P(None, "col", "row", None, None),
            P(None, "col", "row", None, None, None, None),
            P(None, "col", "row", None, None),
        ),
        out_specs=P(None, "col", "row", None, None),
        check_vma=False,
    )
```

```python
import functools

import jax
import jax.numpy as jnp
from jax import lax
from jax.experimental import pallas as pl
from jax.experimental.pallas import tpu as pltpu
from jax.sharding import PartitionSpec as P

MESH = pl.DeviceIdType.MESH
CHUNKS = 2
AHEAD = 1
REACH = (-2, 2, -1, 1)


def kernel(n_col, n_row, rhs, diag, fac, cols, cols_hbm, out, *scratch):
    steps, rows, width = rhs.shape[0], rhs.shape[3], rhs.shape[4]
    slots = fac.shape[4]
    chips = n_col // 2
    half = width // 2
    wide = half // CHUNKS
    fold = max(1, 128 // wide)
    tall = rows // fold
    links = steps - 1

    (rv, dv, fv, cp, own, sent, landed, stage,
     in_loc, in_send, in_recv, z_send, z_recv, c_send, c_recv,
     o_loc, o_send, o_recv) = scratch[:18]
    panels = scratch[18:]

    col = lax.axis_index("col")
    row = lax.axis_index("row")
    core = lax.rem(col, 2)
    chip = lax.div(col, 2)
    partner = col + 1 - 2 * core
    mine = pl.ds(pl.multiple_of(core * half, half), half)
    theirs = pl.ds(pl.multiple_of((1 - core) * half, half), half)

    def to(c, r):
        return {"col": c, "row": r}

    def spans(total):
        return [pl.ds(0, 1), pl.ds(1, total - 1)]

    local = {}
    for g in range(2):
        a, b = spans(steps)[g], spans(links)[g]
        local["rhs", g] = pltpu.make_async_copy(rhs.at[a, 0, 0, :, mine], rv.at[a, 0], in_loc.at[0, g])
        local["diag", g] = pltpu.make_async_copy(diag.at[a, 0, 0], dv.at[a, 0], in_loc.at[1, g])
        local["fac", g] = pltpu.make_async_copy(fac.at[b, 0, 0], fv.at[b, 0], in_loc.at[2, g])
    for c in local.values():
        c.start()

    barrier = pltpu.get_barrier_semaphore()
    pl.semaphore_signal(barrier, inc=1, device_id=to(partner, row), device_id_type=MESH)
    count = chips
    for step in REACH:
        near = (row + step >= 0) & (row + step < n_row)
        count = count + near.astype(jnp.int32)

        @pl.when(near)
        def _():
            pl.semaphore_signal(barrier, inc=1, device_id=to(col, row + step), device_id_type=MESH)

    for d in range(1, chips):
        other = lax.rem(chip + d, chips) * 2 + core
        pl.semaphore_signal(barrier, inc=1, device_id=to(other, row), device_id_type=MESH)
    pl.semaphore_wait(barrier, count)

    def remote(src, dst, send, recv, device):
        return pltpu.make_async_remote_copy(
            src_ref=src, dst_ref=dst, send_sem=send, recv_sem=recv,
            device_id=device, device_id_type=MESH)

    pair = to(partner, row)
    cross = {}
    for g in range(2):
        a, b = spans(steps)[g], spans(links)[g]
        cross["rhs", g] = remote(rhs.at[a, 0, 0, :, theirs], rv.at[a, 1], in_send.at[0, g], in_recv.at[0, g], pair)
        cross["diag", g] = remote(diag.at[a, 0, 0], dv.at[a, 1], in_send.at[1, g], in_recv.at[1, g], pair)
        cross["fac", g] = remote(fac.at[b, 0, 0], fv.at[b, 1], in_send.at[2, g], in_recv.at[2, g], pair)
        if g == 0:
            cross["cols", g] = remote(cols_hbm, cp, in_send.at[3, g], in_recv.at[3, g], pair)
    for c in cross.values():
        c.start()

    def arrived(name, g):
        if (name, g) in local:
            local[name, g].wait()
        cross[name, g].wait_recv()

    def pack(x):
        return x if fold == 1 else jnp.concatenate(
            [x[i * tall:(i + 1) * tall] for i in range(fold)], axis=1)

    def unpack(x):
        return x if fold == 1 else jnp.concatenate(
            [x[:, i * wide:(i + 1) * wide] for i in range(fold)], axis=0)

    def part(ch):
        return pl.ds(ch * wide, wide)

    def z_copy(s, ch, source, step):
        buf = panels[s * CHUNKS + ch]
        way = REACH.index(step)
        return remote(buf.at[source], buf.at[source], z_send.at[s, ch, way, source],
                      z_recv.at[s, ch, source], to(col, row + step))

    def reaches(step):
        return (row + step >= 0) & (row + step < n_row)

    def z_own(s, ch):
        for step in REACH:
            @pl.when(reaches(step))
            def _():
                z_copy(s, ch, row, step).start()

    def hop(s, ch, h):
        if h >= n_row:
            return
        for _ in (0,):
            for step in (-1, 1):
                @pl.when(reaches(-step * h))
                def _():
                    z_copy(s, ch, row - step * h, step).wait_recv()
                    if 2 <= h < n_row - 1:
                        @pl.when(reaches(step))
                        def _():
                            z_copy(s, ch, row - step * h, step).start()

    def z_sent(s, ch):
        for _ in (0,):
            for step in REACH:
                @pl.when(reaches(step))
                def _():
                    z_copy(s, ch, row, step).wait_send()
            for h in range(2, n_row - 1):
                for step in (-1, 1):
                    @pl.when(reaches(step) & reaches(-step * h))
                    def _():
                        z_copy(s, ch, row - step * h, step).wait_send()

    def c_copy(s, ch, d):
        other = lax.rem(chip + d, chips) * 2 + core
        return remote(sent.at[s, ch, d - 1], landed.at[s, ch, d - 1], c_send.at[s, ch, d - 1],
                      c_recv.at[s, ch, d - 1], to(other, row))

    def out_copies(s, ch):
        first, size = (ch + 1 - fold) * wide, fold * wide
        span = pl.ds(pl.multiple_of(core * half + first, size), size)
        src = stage.at[s, :, :, pl.ds(first, size)]
        keep = pltpu.make_async_copy(src.at[0], out.at[s, 0, 0, :, span], o_loc.at[s, ch])
        give = remote(src.at[1], out.at[s, 0, 0, :, span], o_send.at[s, ch], o_recv.at[s, ch], pair)
        return keep, give

    def solve(s, ch):
        if s > 0:
            for d in range(1, chips):
                c_copy(s - 1, ch, d).wait_recv()
        for k in range(2):
            block = dv[s, k]
            right = rv[s, k, :, part(ch)]
            if s == 0:
                x = jnp.dot(block, right, preferred_element_type=jnp.float32)
            else:
                total = own[ch, k]
                for d in range(1, chips):
                    total = total + unpack(landed[s - 1, ch, d - 1, k]).astype(jnp.float32)
                rem = right.astype(jnp.float32) - total
                high = rem.astype(jnp.bfloat16)
                low = (rem - high.astype(jnp.float32)).astype(jnp.bfloat16)
                x = jnp.dot(jnp.concatenate([block, block], axis=1),
                            jnp.concatenate([high, low], axis=0),
                            preferred_element_type=jnp.float32)
            x = x.astype(jnp.bfloat16)
            if s < links:
                panels[s * CHUNKS + ch][row, k] = pack(x)
            stage[s, k, :, part(ch)] = x
        if s < links:
            z_own(s, ch)
        if ch % fold == fold - 1:
            for c in out_copies(s, ch):
                c.start()

    def term(s, ch, other, k):
        buf = panels[s * CHUNKS + ch]
        t = other * 2 + (core if k == 0 else 1 - core)
        left, right = [], []
        for slot, index in ((0, cols), (1, cp)):
            for m in range(slots):
                left.append(fv[s, slot, t, m])
                right.append(unpack(buf[index[s, 0, 0, m, t], slot]))
        return jnp.dot(jnp.concatenate(left, axis=1), jnp.concatenate(right, axis=0),
                       preferred_element_type=jnp.float32)

    def spread(s, ch):
        def one(d):
            other = lax.rem(chip + d, chips)
            for k in range(2):
                sent[s, ch, d - 1, k] = pack(term(s, ch, other, k).astype(jnp.bfloat16))
            c_copy(s, ch, d).start()

        if chips <= 4:
            for d in range(1, chips):
                one(d)
        else:
            @pl.loop(1, chips)
            def _(d):
                one(d)
        for k in range(2):
            own[ch, k] = term(s, ch, chip, k)

    def ready(s, names):
        if s < 2:
            for name in names:
                arrived(name, s)

    for s in range(steps):
        ready(s, ("rhs", "diag"))
        for ch in range(CHUNKS):
            solve(s, ch)
        if s < links:
            ready(s, ("fac", "cols") if s == 0 else ("fac",))
            for ch in range(AHEAD):
                hop(s, ch, 2)
            for ch in range(CHUNKS):
                if ch + AHEAD < CHUNKS:
                    hop(s, ch + AHEAD, 2)
                for h in range(3, n_row):
                    hop(s, ch, h)
                hop(s, ch, 1)
                spread(s, ch)

    for c in cross.values():
        c.wait_send()
    for s in range(steps):
        for ch in range(CHUNKS):
            if ch % fold == fold - 1:
                keep, give = out_copies(s, ch)
                keep.wait()
                give.wait()
            if s < links:
                z_sent(s, ch)
                for d in range(1, chips):
                    c_copy(s, ch, d).wait_send()


def on_device(n_col, n_row, rhs, diag_inv, factor, columns):
    steps, rows, width = rhs.shape[0], rhs.shape[3], rhs.shape[4]
    columns = jnp.swapaxes(columns, 3, 4)
    targets, slots = factor.shape[3], factor.shape[4]
    chips, half = n_col // 2, width // 2
    wide, links = half // CHUNKS, steps - 1
    fold = max(1, 128 // wide)
    packed = (rows // fold, wide * fold)
    bf16 = jnp.bfloat16
    dma = pltpu.SemaphoreType.DMA
    scratch = [
        pltpu.VMEM((steps, 2, rows, half), bf16),
        pltpu.VMEM((steps, 2, rows, rows), bf16),
        pltpu.VMEM((links, 2, targets, slots, rows, rows), bf16),
        pltpu.SMEM(columns.shape, jnp.int32),
        pltpu.VMEM((CHUNKS, 2, rows, wide), jnp.float32),
        pltpu.VMEM((links, CHUNKS, chips - 1, 2) + packed, bf16),
        pltpu.VMEM((links, CHUNKS, chips - 1, 2) + packed, bf16),
        pltpu.VMEM((steps, 2, rows, half), bf16),
        dma((3, 2)), dma((4, 2)), dma((4, 2)),
        dma((links, CHUNKS, len(REACH), n_row)), dma((links, CHUNKS, n_row)),
        dma((links, CHUNKS, chips - 1)), dma((links, CHUNKS, chips - 1)),
        dma((steps, CHUNKS)), dma((steps, CHUNKS)), dma((steps, CHUNKS)),
    ] + [pltpu.VMEM((n_row, 2) + packed, bf16) for _ in range(links * CHUNKS)]
    anywhere = pl.BlockSpec(memory_space=pl.ANY)
    return pl.pallas_call(
        functools.partial(kernel, n_col, n_row),
        out_shape=jax.ShapeDtypeStruct(rhs.shape, bf16),
        in_specs=[anywhere, anywhere, anywhere, pl.BlockSpec(memory_space=pltpu.SMEM), anywhere],
        out_specs=anywhere,
        scratch_shapes=scratch,
        compiler_params=pltpu.CompilerParams(
            collective_id=0, has_side_effects=True, vmem_limit_bytes=60 * 1024 * 1024),
        name="levels",
    )(rhs, diag_inv, factor, columns, columns)


def solution(mesh):
    n_col, n_row = mesh.shape["col"], mesh.shape["row"]
    return jax.shard_map(
        functools.partial(on_device, n_col, n_row),
        mesh=mesh,
        in_specs=(
            P(None, "col", "row", None, None),
            P(None, "col", "row", None, None),
            P(None, "col", "row", None, None, None, None),
            P(None, "col", "row", None, None),
        ),
        out_specs=P(None, "col", "row", None, None),
        check_vma=False,
    )
```
